512 devices in a mesh: ctx: 64 (over z, x_lo, core), head: 8 (over x_hi, y).
Axes of the slice: x: 4 (x_hi: 2, x_lo: 2; x = x_hi * 2 + x_lo), y: 4, z: 16, core: 2. Of those that a mesh axis runs over, the one named last changes fastest.
Arguments:
- queries: bfloat16 [8192, 6144], P('ctx', 'head'), as said below
- keys: bfloat16 [16384, 1024], P('ctx', 'head'), as said below
- values: bfloat16 [16384, 1024], P('ctx', 'head'), may hold values from -6 to 6
- ranges: int32 [4, 2, 2], replicated, may hold values from 0 to 128, as said below
- noise_ids: int32 [4], replicated, may hold values from 0 to 7
- block_position: int32 [128], replicated, may hold values from 0 to 127, as said below
- level_gain: float32 [8, 6144], P(None, 'head'), may hold values from 0.1 to 1.9
Outputs:
- attended: bfloat16 [8192, 6144], P('ctx', 'head')
The draws below stay inside these ranges and needn't reach their ends.
Inputs may be any that keep to these rules, and one draw needn't show every extreme that they name: block_position is a permutation of 0 to 127. Each range has start < end and spans 1 to 64 blocks; some range spans exactly 64; ranges of a stretch may intersect. `queries`: entries of order one in most rows; a draw may hold a few rows whose entries are up to about 28 times larger. `keys`: entries of order one.
All inputs are finite; a program needn't handle non-finite values.
Results may differ from the reference program's by a relative error of at most 0.0075.
Values may be sent and summed in bfloat16 or wider, within the bound.
A program may use at most 64 MiB of HBM per device.

```python
import jax
import jax.numpy as jnp
from jax import lax

D = 6144
KVH = 8
HD = 128
BLK = 128
STRETCHES = 4
NR = 2
LEVELS = 8
GROUP = 6
QTOK = 8192
KTOK = 16384
KBLOCKS = 128
QC = 2048
RSPAN = 64


def make_ranges(key):
    first, second = jax.random.split(jax.random.fold_in(key, 11))
    starts = jax.random.randint(first, (STRETCHES, NR), 0, KBLOCKS - RSPAN + 1)
    spans = jax.random.randint(second, (STRETCHES, NR), 1, RSPAN + 1)
    result = jnp.stack([starts, starts + spans], axis=-1).astype(jnp.int32)
    result = result.at[0, 0].set(jnp.array([0, RSPAN], jnp.int32))
    result = result.at[STRETCHES - 1, NR - 1].set(jnp.array([KBLOCKS - RSPAN, KBLOCKS], jnp.int32))
    return result


def make_positions(key):
    return jax.random.permutation(jax.random.fold_in(key, 12), KBLOCKS).astype(jnp.int32)


def make_pair(key):
    key_base = jnp.clip(jax.random.normal(jax.random.fold_in(key, 13), (KTOK, KVH * HD), jnp.float32), -6.0, 6.0)
    query_base = jnp.clip(jax.random.normal(jax.random.fold_in(key, 14), (QTOK, D), jnp.float32), -6.0, 6.0)
    return (query_base, key_base)


def draw_queries(key, part):
    return make_pair(key)[0].astype(jnp.bfloat16)


def draw_keys(key, part):
    return make_pair(key)[1].astype(jnp.bfloat16)


def draw_ranges(key, part):
    return make_ranges(key)


def draw_block_position(key, part):
    return make_positions(key)


def with_ends(entries, own_key, least, high):
    longest = entries.shape.index(max(entries.shape))
    spots = []
    for shift in (0, 1):
        where = [jax.random.randint(jax.random.fold_in(own_key, axis), (), 0, length) for axis, length in enumerate(entries.shape)]
        where[longest] = (where[longest] + shift) % entries.shape[longest]
        spots.append(tuple(where))
    return entries.at[spots[0]].set(least).at[spots[1]].set(high)


def shard_levels(key, extent, pieces, least, high):
    factor_of = 1.0
    for axis_at, blocks in pieces:
        heights = jax.random.uniform(jax.random.fold_in(jax.random.fold_in(key, 6), axis_at), (blocks,), jnp.float32, least / len(pieces), high / len(pieces))
        factor_of = factor_of * jnp.repeat(jnp.exp(heights), extent[axis_at] // blocks).reshape((-1,) + (1,) * (len(extent) - 1 - axis_at))
    return factor_of


def centred(stream_key, extent, width, reach, shards=(), kind=jnp.bfloat16):
    values = jax.random.normal(stream_key, extent, jnp.float32) * width
    if len(shards) > 0:
        values = shard_levels(stream_key, extent, shards, -0.22, 0.18) * values
    return jnp.clip(values, min=-reach, max=reach).astype(kind)


def setup_inputs(seed: int = 0) -> dict:
    splits = jax.random.split(jax.random.key(seed), 8)
    queries = draw_queries(jax.random.fold_in(splits[7], 71), 0)
    keys = draw_keys(jax.random.fold_in(splits[7], 71), 0)
    values = centred(splits[2], (KTOK, KVH * HD), 1.0, 6.0, ((0, 64), (1, 8)))
    ranges = draw_ranges(jax.random.fold_in(splits[7], 71), 0)
    noise_ids = with_ends(jax.random.randint(splits[4], (STRETCHES,), 0, LEVELS), jax.random.fold_in(splits[4], 1), 0, LEVELS - 1).astype(jnp.int32)
    block_position = draw_block_position(jax.random.fold_in(splits[7], 71), 0)
    level_gain = jnp.clip(1.0 + 0.18 * jax.random.normal(splits[6], (LEVELS, D), jnp.float32), 0.1, 1.9)
    return dict(queries=queries, keys=keys, values=values, ranges=ranges, noise_ids=noise_ids, block_position=block_position, level_gain=level_gain)


def reference(queries, keys, values, ranges, noise_ids, block_position, level_gain):
    score_scale = 1.0 / HD ** 0.5
    logical = block_position[jnp.arange(KTOK) // BLK]
    live_all = jnp.any((logical[None, None, :] >= ranges[:, :, 0:1]) & (logical[None, None, :] < ranges[:, :, 1:2]), axis=1)
    q_block = min(512, QC)
    n_blocks = QTOK // q_block
    keys_heads = keys.reshape(KTOK, KVH, HD).transpose(1, 0, 2)
    values_heads = values.reshape(KTOK, KVH, HD).transpose(1, 0, 2)

    def one_block(index):
        rows = lax.dynamic_slice_in_dim(queries, (index * q_block).astype(jnp.int32), q_block, 0)
        rows = rows.reshape(q_block, KVH, GROUP, HD).transpose(1, 0, 2, 3).reshape(KVH, q_block * GROUP, HD)
        stretch = index * q_block // QC
        live_keys = live_all[stretch]

        def one_head(items):
            query_rows, key_rows, value_rows = items
            score = jnp.dot(query_rows, key_rows.T, preferred_element_type=jnp.float32) * score_scale
            score = jnp.where(live_keys[None, :], score, -1e+30)
            top = lax.optimization_barrier(jnp.max(score, axis=1, keepdims=True))
            weight = jnp.exp(score - top)
            total = lax.optimization_barrier(jnp.sum(weight, axis=1, keepdims=True))
            weight_bf = weight.astype(jnp.bfloat16)
            summed = jnp.dot(weight_bf, value_rows, preferred_element_type=jnp.float32)
            return summed / total
        heads = lax.map(one_head, (rows, keys_heads, values_heads))
        heads = heads.reshape(KVH, q_block, GROUP, HD).transpose(1, 0, 2, 3).reshape(q_block, D)
        square = lax.optimization_barrier(jnp.sum(heads * heads, axis=1, keepdims=True))
        gain_row = level_gain[noise_ids[stretch]]
        return (heads / jnp.sqrt(square / D + 1e-06) * gain_row[None, :]).astype(jnp.bfloat16)
    blocks = lax.map(one_block, jnp.arange(n_blocks, dtype=jnp.int32))
    return blocks.reshape(QTOK, D)
```

```python
import functools

import jax
import jax.numpy as jnp
from jax import lax
from jax.experimental import pallas as pl
from jax.experimental.pallas import tpu as pltpu
from jax.sharding import PartitionSpec as P

D = 6144
HD = 128
BLK = 128
STRETCHES = 4
HEADS = 6
ROWS = 128
OWN = 256
MESH = pl.DeviceIdType.MESH
NEG = -1e30
BIG = 3e38
UNIT = 1.4426950408889634 / HD**0.5


def kernel(
    n_ctx, n_head,
    ranges_ref, noise_ref, pos_ref, q_hbm, k_hbm, v_hbm, gain_ref, out_ref,
    kbuf, vbuf, qall, acc, top, heads, part_out, part_in, lse_out, lse_in, sq_out, sq_in, caps,
    local_sem, ring_send, ring_recv, side_send, side_recv, q_send, q_recv,
    part_send, part_recv, sq_send, sq_recv,
):
    zs = n_ctx // 4
    last = zs // 2
    me = lax.axis_index("ctx")
    head = lax.axis_index("head")
    z = me // 4
    plane = (me // 2) % 2
    core = me % 2
    up = (lax.rem(me + 4, n_ctx), head)
    down = (lax.rem(me + n_ctx - 4, n_ctx), head)
    side = (me + 1 - 2 * core, head)
    twin = (me + 2 - 4 * plane, head)
    peers = [(me, lax.rem(head + j, n_head)) for j in range(1, n_head)]

    barrier = pltpu.get_barrier_semaphore()
    for other in (up, down, side, twin, *peers):
        pl.semaphore_signal(barrier, inc=1, device_id=other, device_id_type=MESH)

    locals_ = [
        pltpu.make_async_copy(k_hbm, kbuf.at[pl.ds(0, OWN)], local_sem.at[0]),
        pltpu.make_async_copy(v_hbm, vbuf.at[pl.ds(0, OWN)], local_sem.at[1]),
    ] + [
        pltpu.make_async_copy(q_hbm.at[:, pl.ds(h * HD, HD)], qall.at[h], local_sem.at[2 + h])
        for h in range(HEADS)
    ]
    for c in locals_:
        c.start()

    def base(d):
        return 512 + (d - 1) * 1024

    def spot(d, way):
        if isinstance(d, int):
            return base(d) + (way * OWN if d < last else 0)
        return base(d) + jnp.where(d < last, way * OWN, 0)

    def shift(d):
        if isinstance(d, int):
            return 512 if d < last else OWN
        return jnp.where(d < last, 512, OWN)

    def rows(start, g):
        start = start + (g % 2) * 128
        if not isinstance(start, int):
            start = pl.multiple_of(start, 128)
        return pl.ds(start, 128)

    def ring(d, way, g):
        buf, hbm = (kbuf, k_hbm) if g < 2 else (vbuf, v_hbm)
        own = isinstance(d, int) and d == 0
        src = hbm.at[pl.ds((g % 2) * 128, 128)] if own else buf.at[rows(spot(d, way), g)]
        return pltpu.make_async_remote_copy(
            src_ref=src,
            dst_ref=buf.at[rows(spot(d + 1, way), g)],
            send_sem=ring_send.at[d, way, g],
            recv_sem=ring_recv.at[d, way, g],
            device_id=(up, down)[way],
            device_id_type=MESH,
        )

    def across(d, way, g):
        buf = kbuf if g < 2 else vbuf
        start = spot(d, way)
        return pltpu.make_async_remote_copy(
            src_ref=buf.at[rows(start, g)],
            dst_ref=buf.at[rows(start + shift(d), g)],
            send_sem=side_send.at[d, way, g],
            recv_sem=side_recv.at[d, way, g],
            device_id=side,
            device_id_type=MESH,
        )

    def across_own(g):
        buf, hbm = ((kbuf, k_hbm), (vbuf, v_hbm))[g]
        return pltpu.make_async_remote_copy(
            src_ref=hbm,
            dst_ref=buf.at[pl.ds(OWN, OWN)],
            send_sem=side_send.at[0, 0, g],
            recv_sem=side_recv.at[0, 0, g],
            device_id=side,
            device_id_type=MESH,
        )

    def query(h):
        return pltpu.make_async_remote_copy(
            src_ref=q_hbm.at[:, pl.ds(h * HD, HD)],
            dst_ref=qall.at[HEADS + h],
            send_sem=q_send.at[h],
            recv_sem=q_recv.at[h],
            device_id=twin,
            device_id_type=MESH,
        )

    def partial(h):
        src, dst = (part_out.at[h], part_in.at[h]) if h < HEADS else (lse_out, lse_in)
        return pltpu.make_async_remote_copy(
            src_ref=src,
            dst_ref=dst,
            send_sem=part_send.at[h],
            recv_sem=part_recv.at[h],
            device_id=twin,
            device_id_type=MESH,
        )

    def square(j):
        return pltpu.make_async_remote_copy(
            src_ref=sq_out,
            dst_ref=sq_in.at[j],
            send_sem=sq_send.at[j],
            recv_sem=sq_recv.at[j],
            device_id=peers[j],
            device_id_type=MESH,
        )

    pl.semaphore_wait(barrier, 4 + n_head - 1)
    for g in range(4):
        for way in (0, 1):
            ring(0, way, g).start()
        if g < 2:
            across_own(g).start()
    for h in range(HEADS):
        query(h).start()

    stretch = me * STRETCHES // n_ctx
    lo0, hi0 = ranges_ref[stretch, 0, 0], ranges_ref[stretch, 0, 1]
    lo1, hi1 = ranges_ref[stretch, 1, 0], ranges_ref[stretch, 1, 1]

    def cap(b, carry):
        far = b - 4
        d = jnp.where(b < 4, 0, far // 8 + 1)
        r = jnp.where(b < 4, b, far % 8)
        short = jnp.logical_or(b < 4, d == last)
        other = jnp.where(short, r // 2, r // 4)
        way = jnp.where(short, 0, (r // 2) % 2)
        from_z = lax.rem(z + zs + jnp.where(way == 0, -d, d), zs)
        device = from_z * 4 + plane * 2 + lax.rem(core + other, 2)
        at = pos_ref[device * 2 + b % 2]
        live = ((at >= lo0) & (at < hi0)) | ((at >= lo1) & (at < hi1))
        caps[b] = jnp.where(live, BIG, NEG).astype(jnp.float32)
        return carry

    lax.fori_loop(0, zs * 4, cap, 0)

    def scores(t, start, n):
        return lax.dot_general(
            qall[t], kbuf[pl.ds(start, n), :], (((1,), (1,)), ((), ())),
            preferred_element_type=jnp.float32,
        )

    def weigh(t, s, limits, first):
        xs = [
            jnp.minimum(s[:, 128 * j : 128 * j + 128], c) for j, c in enumerate(limits)
        ]
        tree = xs
        while len(tree) > 1:
            tree = [
                jnp.maximum(*tree[i : i + 2]) if i + 1 < len(tree) else tree[i]
                for i in range(0, len(tree), 2)
            ]
        new = jnp.broadcast_to(jnp.max(tree[0], axis=1, keepdims=True), (ROWS, 128))
        if first:
            fade = None
        else:
            old = top[t]
            new = jnp.maximum(old, new)
            fade = jnp.exp2((old - new) * UNIT)
        top[t] = new
        ps = [jnp.exp2((x - new) * UNIT).astype(jnp.bfloat16) for x in xs]
        return jnp.concatenate(ps, axis=1), fade

    def gather(t, p, fade, start, n):
        ones = jnp.ones((n, 128), jnp.bfloat16)
        v = jnp.concatenate([vbuf[pl.ds(start, n), :], ones], axis=1)
        o = jnp.dot(p, v, preferred_element_type=jnp.float32)
        if fade is None:
            acc[t] = o
        else:
            a = acc[t]
            acc[t, :, :128] = a[:, :128] * fade + o[:, :128]
            acc[t, :, 128:] = a[:, 128:] * fade + o[:, 128:]

    def attend(tiles, start, n, before=lambda i: None, after=lambda i: None, first=False):
        at = start // 128
        limits = [caps[at + j] for j in range(n // 128)]
        s, p = {}, {}
        for i in range(len(tiles) + 1):
            if i == 0:
                before(0)
                s[0] = scores(tiles[0], start, n)
            if i + 1 < len(tiles):
                before(i + 1)
                s[i + 1] = scores(tiles[i + 1], start, n)
            if i < len(tiles):
                p[i] = weigh(tiles[i], s.pop(i), limits, first)
            if i >= 1:
                gather(tiles[i - 1], *p.pop(i - 1), start, n)
                after(i - 1)

    def step(d, g):
        for way in (0, 1):
            half = (way == 0) == (g < 2)

            def take(way=way):
                ring(d - 1, way, g).wait_recv()

            def on(way=way):
                ring(d, way, g).start()

            def over(way=way):
                across(d, way, g).start()

            if isinstance(d, int):
                if half or d < last:
                    take()
                    if d < (last if half else last - 1):
                        on()
                    over()
            elif half:
                take()
                pl.when(d < last)(on)
                over()
            else:

                @pl.when(d < last)
                def _():
                    take()
                    pl.when(d < last - 1)(on)
                    over()

    def settle(d):
        for g in range(4):
            for way in (0, 1):
                if isinstance(d, int) and d == last and (way == 0) != (g < 2):
                    continue
                across(d, way, g).wait_recv()

    own_tiles = list(range(HEADS))
    twin_tiles = list(range(HEADS, 2 * HEADS))
    for c in locals_:
        c.wait()
    for g in (0, 1):
        across_own(g).wait_recv()
    attend(own_tiles, 0, 512, first=True)
    for g in range(4):
        step(1, g)
    attend(twin_tiles, 0, 512, before=lambda i: query(i).wait_recv(), first=True)

    def turn(d, carry):
        settle(d - 1)

        def before(i):
            if i % 3 == 0:
                step(d, i // 3)

        attend(
            own_tiles + twin_tiles, pl.multiple_of(base(d - 1), 128), 1024, before=before
        )
        return carry

    lax.fori_loop(2, last + 1, turn, 0)

    settle(last)
    lane = lax.broadcasted_iota(jnp.int32, (ROWS, 128), 1)
    lse = [jnp.zeros((ROWS, 128), jnp.float32)]

    def finish(i):
        if i >= HEADS:
            return
        t = twin_tiles[i]
        total = acc[t, :, 128:]
        part_out[i] = (acc[t, :, :128] / total).astype(jnp.bfloat16)
        lse[0] = jnp.where(lane == i, top[t] * UNIT + jnp.log2(total), lse[0])
        if i == HEADS - 1:
            lse_out[...] = lse[0].T[0:8, :]

    def send(i):
        finish(i)
        if 1 <= i <= HEADS + 1:
            partial(i - 1).start()

    attend(twin_tiles + own_tiles, base(last), 512, after=send)

    square_here = jnp.zeros((ROWS, 128), jnp.float32)
    partial(HEADS).wait_recv()
    lse_cols = jnp.concatenate([lse_in[...], jnp.zeros((120, 128), jnp.float32)], axis=0).T
    for h in range(HEADS):
        partial(h).wait_recv()
        there = jnp.broadcast_to(lse_cols[:, h : h + 1], (ROWS, 128))
        here = top[h] * UNIT
        high = jnp.maximum(here, there)
        a, b = jnp.exp2(here - high), jnp.exp2(there - high)
        both = acc[h, :, 128:] * a + b
        value = (acc[h, :, :128] * a + part_in[h].astype(jnp.float32) * b) / both
        heads[h] = value
        square_here = square_here + value * value
    square_here = jnp.broadcast_to(
        jnp.sum(square_here, axis=1, keepdims=True), (ROWS, 128)
    ).T[0:8, :]
    sq_out[...] = square_here

    for g in range(4):
        for way in (0, 1):
            ring(0, way, g).wait_send()
        if g < 2:
            across_own(g).wait_send()
    for j in range(n_head - 1):
        square(j).start()
    for h in range(HEADS):
        query(h).wait_send()
    for h in range(HEADS + 1):
        partial(h).wait_send()

    def sent(d, carry):
        for g in range(4):
            for way in (0, 1):
                across(d, way, g).wait_send()

                @pl.when(jnp.logical_or(d < last - 1, (way == 0) == (g < 2)))
                def _():
                    ring(d, way, g).wait_send()

        return carry

    lax.fori_loop(1, last, sent, 0)
    for g in range(4):
        across(last, 0 if g < 2 else 1, g).wait_send()

    level = noise_ref[stretch]
    gain = gain_ref[pl.ds(level, 1), :]
    square_all = square_here
    for j in range(n_head - 1):
        square(j).wait_recv()
        square_all = square_all + sq_in[j]
    scale = 1.0 / jnp.sqrt(square_all / (HEADS * HD * n_head) + 1e-06)
    scale = jnp.broadcast_to(scale[0:1, :], (128, 128)).T
    for h in range(HEADS):
        out_ref[:, h * HD : (h + 1) * HD] = (
            heads[h] * scale * gain[:, h * HD : (h + 1) * HD]
        ).astype(out_ref.dtype)
    for j in range(n_head - 1):
        square(j).wait_send()


def body(n_ctx, n_head, queries, keys, values, ranges, noise_ids, block_position, level_gain):
    last = n_ctx // 8
    smem = pl.BlockSpec(memory_space=pltpu.SMEM)
    vmem = pl.BlockSpec(memory_space=pltpu.VMEM)
    anywhere = pl.BlockSpec(memory_space=pl.ANY)
    dma = pltpu.SemaphoreType.DMA
    return pl.pallas_call(
        functools.partial(kernel, n_ctx, n_head),
        out_shape=jax.ShapeDtypeStruct((ROWS, HEADS * HD), jnp.bfloat16),
        in_specs=[smem, smem, smem, anywhere, anywhere, anywhere, vmem],
        out_specs=vmem,
        scratch_shapes=[
            pltpu.VMEM((last * 1024, HD), jnp.bfloat16),
            pltpu.VMEM((last * 1024, HD), jnp.bfloat16),
            pltpu.VMEM((2 * HEADS, ROWS, HD), jnp.bfloat16),
            pltpu.VMEM((2 * HEADS, ROWS, 256), jnp.float32),
            pltpu.VMEM((2 * HEADS, ROWS, 128), jnp.float32),
            pltpu.VMEM((HEADS, ROWS, HD), jnp.float32),
            pltpu.VMEM((HEADS, ROWS, HD), jnp.bfloat16),
            pltpu.VMEM((HEADS, ROWS, HD), jnp.bfloat16),
            pltpu.VMEM((8, 128), jnp.float32),
            pltpu.VMEM((8, 128), jnp.float32),
            pltpu.VMEM((8, 128), jnp.float32),
            pltpu.VMEM((n_head - 1, 8, 128), jnp.float32),
            pltpu.SMEM((last * 8,), jnp.float32),
            dma((2 + HEADS,)),
            dma((last, 2, 4)),
            dma((last, 2, 4)),
            dma((last + 1, 2, 4)),
            dma((last + 1, 2, 4)),
            dma((HEADS,)),
            dma((HEADS,)),
            dma((HEADS + 1,)),
            dma((HEADS + 1,)),
            dma((n_head - 1,)),
            dma((n_head - 1,)),
        ],
        compiler_params=pltpu.CompilerParams(
            collective_id=0, has_side_effects=True, vmem_limit_bytes=48 << 20
        ),
        name="attend",
    )(ranges, noise_ids, block_position, queries, keys, values, level_gain)


def solution(mesh):
    placed = (P("ctx", "head"), P("ctx", "head"), P("ctx", "head"), P(), P(), P(), P(None, "head"))
    return jax.shard_map(
        functools.partial(body, mesh.shape["ctx"], mesh.shape["head"]),
        mesh=mesh, in_specs=placed, out_specs=P("ctx", "head"), check_vma=False,
    )
```
